32 devices in a mesh: tm: 2 (over core), space: 16 (over z, y, x).
Axes of the slice: x: 2, y: 2, z: 4, core: 2. Of those that a mesh axis runs over, the one named last changes fastest.
Arguments:
- checkpoints: float32 [2, 5, 2048, 128], P('tm', None, 'space'), may hold values from -6 to 6
- sources: float32 [2, 5, 2048, 128], P(None, None, 'space'), may hold values from -3 to 3
- pitch: float32 [8], replicated, may hold values from -3.140625 to 3.140625
- metric: float32 [2048, 128], P('space'), may hold values from 0.5 to 2
- obj_weight: float32 [5, 2048, 128], P(None, 'space'), may hold values from 0.1 to 0.6
- adjoint_end: float32 [5, 2048, 128], P(None, 'space'), may hold values from -6 to 6
- lift: bfloat16 [5, 128, 128], replicated, may hold values from -0.5 to 0.5
- mixing: float32 [5, 5, 5], replicated, may hold values from -1.25 to 1.25
- faces: int32 [2048, 4], P('space'), may hold values from 0 to 191
- send_idx: int32 [16, 4, 16], P('space'), may hold values from 0 to 127
Outputs:
- adjoint_bounds: float32 [2, 5, 2048, 128], P('tm', None, 'space')
- pitch_grad: float32 [8], replicated
The draws below stay inside these ranges and needn't reach their ends.
Inputs may be any that keep to these rules, and one draw needn't show every extreme that they name: `faces`: values below 128 name the subdomain's own blocks; value 128 + d * 16 + s names slot s of the blocks received from direction d. `send_idx`: entry [p, d, s] is a local block of subdomain p sent to subdomain p + o[d], o = (1, -1, 2, -2); blocks may repeat.
All inputs are finite; a program needn't handle non-finite values.
Results may differ from the reference program's by a relative error of at most 0.0035.
Values may be sent and summed in bfloat16 or wider, within the bound.
No kernel may reach another device: no remote copies, remote signals or barrier semaphores. Data moves between devices by JAX's collectives and lax.ppermute only.
A program may use at most 64 MiB of HBM per device.

```python
import math
import jax
import jax.numpy as jnp
from jax import lax

COMPS = 5
NODES = 128
FACES = 4
LEVELS = 8
BLK_DEV = 128
HALO = 16
NBT = 2048
N_TM = 2
N_SPACE = 16


def with_ends(drawn, key, least, high):
    extent = drawn.shape
    spot = [jax.random.randint(jax.random.fold_in(key, axis), (), 0, extent[axis]) for axis in range(len(extent))]
    drawn = drawn.at[tuple(spot)].set(least)
    longest = extent.index(max(extent))
    spot[longest] = (spot[longest] + 1) % extent[longest]
    return drawn.at[tuple(spot)].set(high)


def level_of(rng, extent, cuts, low, largest):
    factor_of, own = 1.0, jax.random.fold_in(rng, 6)
    for position, blocks in cuts:
        steps = jnp.exp(jax.random.uniform(jax.random.fold_in(own, position), (blocks,), jnp.float32, low / len(cuts), largest / len(cuts)))
        factor_of = factor_of * jnp.repeat(steps, extent[position] // blocks).reshape([-1 if axis == position else 1 for axis in range(len(extent))])
    return factor_of


def noise(rng, dims, spread, limit, cuts=(), held_as=jnp.bfloat16):
    entries = jax.random.normal(rng, dims, jnp.float32) * spread
    if len(cuts) > 0:
        entries = level_of(rng, dims, cuts, -0.22, 0.18) * entries
    return jnp.clip(entries, min=-limit, max=limit).astype(held_as)


def setup_inputs(seed: int = 0) -> dict:
    key_of = jax.random.split(jax.random.key(seed), 11)
    return {
        "checkpoints": noise(key_of[0], (2, COMPS, NBT, NODES), 1.0, 6.0, ((0, 2), (2, 16)), jnp.float32),
        "sources": noise(key_of[1], (2, COMPS, NBT, NODES), 0.5, 3.0, ((2, 16),), jnp.float32),
        "pitch": jnp.clip(jax.random.uniform(key_of[2], (LEVELS,), jnp.float32, -3.140625, 3.140625), -3.140625, 3.140625),
        "metric": jnp.clip(jnp.exp(math.log(2.0) - 1.3862944 * jax.random.uniform(key_of[3], (NBT, NODES), jnp.float32) ** level_of(key_of[3], (NBT, NODES), ((0, 16),), -0.2, 0.2)), 0.5, 2.0),
        "obj_weight": jnp.clip(0.1 + 0.5 * jax.random.uniform(key_of[4], (COMPS, NBT, NODES), jnp.float32) ** level_of(key_of[4], (COMPS, NBT, NODES), ((1, 16),), -0.2, 0.2), 0.1, 0.6),
        "adjoint_end": noise(key_of[5], (COMPS, NBT, NODES), 1.0, 6.0, ((1, 16),), jnp.float32),
        "lift": noise(key_of[6], (FACES + 1, NODES, NODES), NODES ** -0.5, 0.5),
        "mixing": noise(key_of[7], (FACES + 1, COMPS, COMPS), (COMPS * (FACES + 1)) ** -0.5, 1.25, (), jnp.float32),
        "faces": with_ends(jax.random.randint(key_of[8], (NBT, FACES), 0, BLK_DEV + 4 * HALO), jax.random.fold_in(key_of[8], 1), 0, (BLK_DEV + 4 * HALO) - 1).astype(jnp.int32),
        "send_idx": with_ends(jax.random.randint(key_of[9], (N_SPACE, 4, HALO), 0, BLK_DEV), jax.random.fold_in(key_of[9], 1), 0, BLK_DEV - 1).astype(jnp.int32),
    }


OFFSETS = (1, -1, 2, -2)
STEP_SIZE = 0.5

def global_faces(faces, send_idx):
    total_blocks = faces.shape[0]
    blk_count = total_blocks // N_SPACE
    slot_count = send_idx.shape[2]
    owner_dev = (jnp.arange(total_blocks, dtype=jnp.int32) // blk_count)[:, None]
    inside = owner_dev * blk_count + faces
    beyond = jnp.maximum(faces - blk_count, 0)
    direction = beyond // slot_count
    slot_pos = beyond % slot_count
    shifts = jnp.array(OFFSETS, dtype=jnp.int32)[direction]
    source_dev = owner_dev - shifts
    is_valid = (source_dev >= 0) & (source_dev < N_SPACE)
    clipped = jnp.clip(source_dev, 0, N_SPACE - 1)
    flat_send = send_idx.reshape(-1)
    picked = flat_send[(clipped * 4 + direction) * slot_count + slot_pos]
    outside = jnp.where(is_valid, clipped * blk_count + picked, total_blocks)
    return jnp.where(faces < blk_count, inside, outside).astype(jnp.int32)

def residual_of(current, global_index, metric, lift_float, mixing):
    squashed = lax.optimization_barrier(jnp.tanh(current).astype(jnp.bfloat16))
    squashed = squashed.astype(jnp.float32)
    padded = jnp.concatenate([squashed, jnp.zeros((COMPS, 1, NODES), jnp.float32)], axis=1)
    totals = jnp.zeros(current.shape, jnp.float32)
    for face_slot in range(global_index.shape[1]):
        picked = padded[:, global_index[:, face_slot], :]
        products = jnp.einsum('cbj,ij->cbi', picked, lift_float[face_slot], precision=lax.Precision.HIGHEST)
        totals = totals + jnp.einsum('ec,cbi->ebi', mixing[face_slot], products, precision=lax.Precision.HIGHEST)
    return metric[None] * totals

def transpose_of(adjoint, current, global_index, metric, lift_float, mixing):
    total_blocks = current.shape[1]
    weighted = metric[None] * adjoint
    totals = jnp.zeros((COMPS, total_blocks + 1, NODES), jnp.float32)
    for face_slot in range(global_index.shape[1]):
        mixed = jnp.einsum('ec,ebi->cbi', mixing[face_slot], weighted, precision=lax.Precision.HIGHEST)
        mixed = lax.optimization_barrier(mixed.astype(jnp.bfloat16)).astype(jnp.float32)
        returned_terms = jnp.einsum('cbi,ij->cbj', mixed, lift_float[face_slot], precision=lax.Precision.HIGHEST)
        totals = totals.at[:, global_index[:, face_slot], :].add(returned_terms)
    derivative = 1.0 - jnp.tanh(current) ** 2
    return totals[:, :total_blocks, :] * derivative

def reference(checkpoints, sources, pitch, metric, obj_weight, adjoint_end, lift, mixing, faces, send_idx):
    total_blocks = faces.shape[0]
    own_index = jnp.arange(total_blocks, dtype=jnp.int32)[:, None]
    global_index = jnp.concatenate([own_index, global_faces(faces, send_idx)], axis=1).astype(jnp.int32)
    half_count = LEVELS // N_TM
    lift_float = lift.astype(jnp.float32)
    states = []
    current = checkpoints[0]
    for segment in range(N_TM):
        current = checkpoints[segment]
        for within in range(half_count):
            level_now = segment * half_count + within
            states.append(current)
            forcing = jnp.cos(pitch[level_now]) * sources[0] + jnp.sin(pitch[level_now]) * sources[1]
            current = current + STEP_SIZE * (forcing - residual_of(current, global_index, metric, lift_float, mixing))
    states.append(current)
    normalizer = math.sqrt(COMPS * NODES * total_blocks)
    adjoint = adjoint_end + obj_weight * states[LEVELS]
    grads = [None] * LEVELS
    bounds = [None, None]
    for level_now in reversed(range(LEVELS)):
        turning = jnp.cos(pitch[level_now]) * sources[1] - jnp.sin(pitch[level_now]) * sources[0]
        grads[level_now] = STEP_SIZE * jnp.sum(adjoint * turning) / normalizer
        adjoint = adjoint - STEP_SIZE * transpose_of(adjoint, states[level_now], global_index, metric, lift_float, mixing)
        if level_now > 0:
            adjoint = adjoint + obj_weight * states[level_now]
        if level_now % half_count == 0:
            bounds[level_now // half_count] = adjoint
    return (jnp.stack(bounds), jnp.stack(grads))
```

```python
import functools
import math

import jax
import jax.numpy as jnp
from jax import lax
from jax.experimental import pallas as pl
from jax.experimental.pallas import tpu as pltpu
from jax.sharding import PartitionSpec as P

OFFSETS = (1, -1, 2, -2)
STEP_SIZE = 0.5
CHUNK = 32
F32 = jnp.float32
BF16 = jnp.bfloat16


def mm(x, y):
    return lax.dot_general(x, y, (((1,), (0,)), ((), ())), preferred_element_type=F32)


def mm_t(x, y):
    return lax.dot_general(x, y, (((1,), (1,)), ((), ())), preferred_element_type=F32)


def chunks(blocks, body):
    step = math.gcd(blocks, CHUNK)

    def run(i, carry):
        return body(pl.ds(pl.multiple_of(i * step, step), step), carry)

    return functools.partial(lax.fori_loop, 0, blocks // step, run)


def emit_packets(send_hot, squashed, packets):
    halo = packets[0].shape[0]
    sent = mm(send_hot[...], squashed[...]).astype(BF16)
    for d, packet in enumerate(packets):
        packet[...] = sent[d * halo : (d + 1) * halo]


def first_kernel(state, send_hot, squashed, *packets):
    comps, _, nodes = state.shape
    for c in range(comps):
        squashed[:, c * nodes : (c + 1) * nodes] = jnp.tanh(state[c]).astype(BF16)
    emit_packets(send_hot, squashed, packets)


def residual_products(squashed, received, gather_hot, lift, products):
    blocks = squashed.shape[0]
    slots, nodes, _ = lift.shape
    comps = squashed.shape[1] // nodes
    own = squashed[...]
    extended = jnp.concatenate([own] + [r[...] for r in received], axis=0)
    picked = mm(gather_hot[...], extended).astype(BF16)
    for k in range(slots):
        rows = own if k == 0 else picked[(k - 1) * blocks : k * blocks]
        stacked = jnp.concatenate([rows[:, c * nodes : (c + 1) * nodes] for c in range(comps)], axis=0)
        products[k] = mm_t(stacked, lift[k]).reshape(comps, blocks, nodes)


def stepped(rows, turn, mixing, state, sources, metric, products):
    slots, comps = products.shape[0], products.shape[1]
    totals = [None] * comps
    for k in range(slots):
        for c in range(comps):
            term = products[k, c, rows, :]
            for e in range(comps):
                part = mixing[(k * comps + e) * comps + c] * term
                totals[e] = part if totals[e] is None else totals[e] + part
    scale = metric[rows, :]
    return [
        state[e, rows, :]
        + STEP_SIZE
        * (turn[0] * sources[0, e, rows, :] + turn[1] * sources[1, e, rows, :] - scale * totals[e])
        for e in range(comps)
    ]


def forward_kernel(
    turn, mixing, state, squashed_in, r0, r1, r2, r3, sources, metric, lift, gather_hot, send_hot,
    next_state, squashed, p0, p1, p2, p3, products,
):
    comps, blocks, nodes = state.shape
    residual_products(squashed_in, (r0, r1, r2, r3), gather_hot, lift, products)

    def body(rows, carry):
        fresh = stepped(rows, turn, mixing, state, sources, metric, products)
        for e in range(comps):
            next_state[e, rows, :] = fresh[e]
            squashed[rows, e * nodes : (e + 1) * nodes] = jnp.tanh(fresh[e]).astype(BF16)
        return carry

    chunks(blocks, body)(0)
    emit_packets(send_hot, squashed, (p0, p1, p2, p3))


def mix_back(rows, turn, mixing, adjoint, sources, metric, mixed, grad):
    slots, comps = mixed.shape[0], mixed.shape[1]
    scale = metric[rows, :]
    for e in range(comps):
        turning = turn[0] * sources[1, e, rows, :] - turn[1] * sources[0, e, rows, :]
        part = adjoint[e] * turning
        grad = grad + part.reshape(-1, 8, part.shape[-1]).sum(axis=0)
    weighted = [scale * adjoint[e] for e in range(comps)]
    for k in range(slots):
        for c in range(comps):
            total = mixing[k * comps * comps + c] * weighted[0]
            for e in range(1, comps):
                total = total + mixing[(k * comps + e) * comps + c] * weighted[e]
            mixed[k, c, rows, :] = total.astype(BF16)
    return grad


def push_back(mixed, lift, scatter_hot, terms, local_part, packets):
    slots, comps, blocks, nodes = mixed.shape
    halo = packets[0].shape[0]
    own = None
    for k in range(slots):
        product = mm(mixed[k].reshape(comps * blocks, nodes), lift[k])
        if k == 0:
            own = product
            continue
        for c in range(comps):
            terms[(k - 1) * blocks : k * blocks, c * nodes : (c + 1) * nodes] = product[
                c * blocks : (c + 1) * blocks
            ].astype(BF16)
    totals = mm(scatter_hot[...], terms[...])
    for c in range(comps):
        local_part[:, c * nodes : (c + 1) * nodes] = (
            totals[:blocks, c * nodes : (c + 1) * nodes] + own[c * blocks : (c + 1) * blocks]
        )
    for d, packet in enumerate(packets):
        packet[...] = totals[blocks + d * halo : blocks + (d + 1) * halo].astype(BF16)


def turn_kernel(
    turn, mixing, state, squashed_in, r0, r1, r2, r3, sources, metric, weight, adjoint_end, lift,
    gather_hot, scatter_hot, adjoint, grad, local_part, p0, p1, p2, p3, products, mixed, terms,
):
    comps, blocks, nodes = state.shape
    residual_products(squashed_in, (r0, r1, r2, r3), gather_hot, lift, products)

    def body(rows, carry):
        fresh = stepped(rows, turn, mixing, state, sources, metric, products)
        values = [adjoint_end[e, rows, :] + weight[e, rows, :] * fresh[e] for e in range(comps)]
        for e in range(comps):
            adjoint[e, rows, :] = values[e]
        return mix_back(rows, turn, mixing, values, sources, metric, mixed, carry)

    grad[...] = chunks(blocks, body)(jnp.zeros(grad.shape, F32))
    push_back(mixed, lift, scatter_hot, terms, local_part, (p0, p1, p2, p3))


def start_kernel(
    turn, mixing, adjoint, sources, metric, lift, scatter_hot,
    grad, local_part, p0, p1, p2, p3, mixed, terms,
):
    comps, blocks, nodes = adjoint.shape

    def body(rows, carry):
        values = [adjoint[e, rows, :] for e in range(comps)]
        return mix_back(rows, turn, mixing, values, sources, metric, mixed, carry)

    grad[...] = chunks(blocks, body)(jnp.zeros(grad.shape, F32))
    push_back(mixed, lift, scatter_hot, terms, local_part, (p0, p1, p2, p3))


def finished(rows, keep, adjoint_in, pushed, state, weight):
    comps, _, nodes = adjoint_in.shape
    values = []
    for e in range(comps):
        now = state[e, rows, :]
        bent = jnp.tanh(now)
        values.append(
            adjoint_in[e, rows, :]
            - STEP_SIZE * (pushed[rows, e * nodes : (e + 1) * nodes] * (1.0 - bent * bent))
            + keep * (weight[e, rows, :] * now)
        )
    return values


def add_returned(local_in, received, return_hot, pushed):
    returned = jnp.concatenate([r[...] for r in received], axis=0)
    pushed[...] = local_in[...] + mm(return_hot[...], returned)


def reverse_kernel(
    turn, mixing, adjoint_in, local_in, r0, r1, r2, r3, state, weight, sources, metric, lift,
    scatter_hot, return_hot, adjoint, grad, local_part, p0, p1, p2, p3, pushed, mixed, terms,
):
    comps, blocks, nodes = state.shape
    add_returned(local_in, (r0, r1, r2, r3), return_hot, pushed)

    def body(rows, carry):
        values = finished(rows, 1.0, adjoint_in, pushed, state, weight)
        for e in range(comps):
            adjoint[e, rows, :] = values[e]
        return mix_back(rows, turn, mixing, values, sources, metric, mixed, carry)

    grad[...] = chunks(blocks, body)(jnp.zeros(grad.shape, F32))
    push_back(mixed, lift, scatter_hot, terms, local_part, (p0, p1, p2, p3))


def last_kernel(keep, adjoint_in, local_in, r0, r1, r2, r3, state, weight, return_hot, adjoint, pushed):
    comps, blocks, nodes = state.shape
    add_returned(local_in, (r0, r1, r2, r3), return_hot, pushed)

    def body(rows, carry):
        values = finished(rows, keep[0], adjoint_in, pushed, state, weight)
        for e in range(comps):
            adjoint[e, rows, :] = values[e]
        return carry

    chunks(blocks, body)(0)


def call(kernel, scalars, arrays, outs, scratch=()):
    smem = pl.BlockSpec(memory_space=pltpu.SMEM)
    vmem = pl.BlockSpec(memory_space=pltpu.VMEM)
    return pl.pallas_call(
        kernel,
        out_shape=outs,
        in_specs=[smem] * len(scalars) + [vmem] * len(arrays),
        out_specs=[vmem] * len(outs),
        scratch_shapes=[pltpu.VMEM(shape, dtype) for shape, dtype in scratch],
        compiler_params=pltpu.CompilerParams(vmem_limit_bytes=16 * 1024 * 1024),
        name=kernel.__name__,
    )(*scalars, *arrays)


def swap(packets, sign):
    devices = range(lax.axis_size("space"))
    received = []
    for packet, offset in zip(packets, OFFSETS):
        route = [(i - sign * offset, i) for i in devices if i - sign * offset in devices]
        received.append(lax.ppermute(packet, "space", route))
    return received


def shards(
    checkpoints, sources, pitch, metric, obj_weight, adjoint_end, lift, mixing, faces, send_idx
):
    comps, blocks, nodes = adjoint_end.shape
    slots = lift.shape[0]
    group = lax.axis_index("tm")
    groups = lax.axis_size("tm")
    count = pitch.shape[0] // groups
    halo = send_idx.shape[2]
    wide = comps * nodes
    extent = blocks + len(OFFSETS) * halo
    normalizer = math.sqrt(comps * nodes * blocks * lax.axis_size("space"))

    senders = send_idx.reshape(-1)
    named = faces.T.reshape(-1)
    gather_hot = (named[:, None] == jnp.arange(extent, dtype=jnp.int32)[None, :]).astype(BF16)
    scatter_hot = (named[None, :] == jnp.arange(extent, dtype=jnp.int32)[:, None]).astype(BF16)
    send_hot = (senders[:, None] == jnp.arange(blocks, dtype=jnp.int32)[None, :]).astype(BF16)
    return_hot = (senders[None, :] == jnp.arange(blocks, dtype=jnp.int32)[:, None]).astype(BF16)
    own_pitch = lax.dynamic_slice_in_dim(pitch, group * count, count)
    turns = [jnp.stack([jnp.cos(own_pitch[n]), jnp.sin(own_pitch[n])]) for n in range(count)]
    mix_flat = mixing.reshape(-1)
    keep = (group > 0).astype(F32).reshape(1)

    def shape(dims, dtype=F32):
        return jax.ShapeDtypeStruct(dims, dtype)

    packet_shapes = [shape((halo, wide), BF16)] * len(OFFSETS)
    state_shape = shape((comps, blocks, nodes))
    reverse_shapes = [shape((8, nodes)), shape((blocks, wide))] + packet_shapes
    product_scratch = ((slots, comps, blocks, nodes), F32)
    push_scratch = [((slots, comps, blocks, nodes), BF16), (((slots - 1) * blocks, wide), BF16)]
    pushed_scratch = ((blocks, wide), F32)

    state = checkpoints[0]
    states = [state]
    squashed, *packets = call(
        first_kernel, (), (state, send_hot), [shape((blocks, wide), BF16)] + packet_shapes
    )
    for n in range(count - 1):
        received = swap(packets, 1)
        state, squashed, *packets = call(
            forward_kernel, (turns[n], mix_flat),
            (state, squashed, *received, sources, metric, lift, gather_hot, send_hot),
            [state_shape, shape((blocks, wide), BF16)] + packet_shapes, [product_scratch],
        )
        states.append(state)
    received = swap(packets, 1)
    adjoint, grad, local_part, *packets = call(
        turn_kernel, (turns[count - 1], mix_flat),
        (state, squashed, *received, sources, metric, obj_weight, adjoint_end, lift, gather_hot,
         scatter_hot),
        [state_shape] + reverse_shapes, [product_scratch] + push_scratch,
    )
    grads = [None] * count
    bound = None
    for phase in reversed(range(groups)):
        mine = group == phase
        if phase < groups - 1:
            adjoint = lax.ppermute(adjoint, "tm", [(phase + 1, phase)])
            grad, local_part, *packets = call(
                start_kernel, (turns[count - 1], mix_flat),
                (adjoint, sources, metric, lift, scatter_hot), reverse_shapes, push_scratch,
            )
        for n in reversed(range(count)):
            grads[n] = grad if grads[n] is None else jnp.where(mine, grad, grads[n])
            received = swap(packets, -1)
            if n > 0:
                adjoint, grad, local_part, *packets = call(
                    reverse_kernel, (turns[n - 1], mix_flat),
                    (adjoint, local_part, *received, states[n], obj_weight, sources, metric, lift,
                     scatter_hot, return_hot),
                    [state_shape] + reverse_shapes, [pushed_scratch] + push_scratch,
                )
            else:
                (adjoint,) = call(
                    last_kernel, (keep,),
                    (adjoint, local_part, *received, states[0], obj_weight, return_hot),
                    [state_shape], [pushed_scratch],
                )
        bound = adjoint if bound is None else jnp.where(mine, adjoint, bound)
    partial_value = jnp.stack([jnp.sum(g) for g in grads]) * (STEP_SIZE / normalizer)
    every = lax.all_gather(partial_value, ("tm", "space"), axis=0, tiled=False)
    values = every.reshape(groups, -1, count).sum(axis=1).reshape(-1)
    return (bound[None], values)


def solution(mesh):
    placed = (
        P("tm", None, "space", None),
        P(None, None, "space", None),
        P(),
        P("space", None),
        P(None, "space", None),
        P(None, "space", None),
        P(),
        P(),
        P("space", None),
        P("space", None, None),
    )
    return jax.shard_map(
        shards,
        mesh=mesh,
        in_specs=placed,
        out_specs=(P("tm", None, "space", None), P()),
        check_vma=False,
    )
```

```python
import functools
import math

import jax
import jax.numpy as jnp
from jax import lax
from jax.experimental import pallas as pl
from jax.experimental.pallas import tpu as pltpu
from jax.sharding import PartitionSpec as P

OFFSETS = (1, -1, 2, -2)
STEP_SIZE = 0.5
CHUNK = 32
F32 = jnp.float32
BF16 = jnp.bfloat16


def mm(x, y):
    return lax.dot_general(x, y, (((1,), (0,)), ((), ())), preferred_element_type=F32)


def mm_t(x, y):
    return lax.dot_general(x, y, (((1,), (1,)), ((), ())), preferred_element_type=F32)


def chunks(blocks, body):
    step = math.gcd(blocks, CHUNK)

    def run(i, carry):
        return body(pl.ds(pl.multiple_of(i * step, step), step), carry)

    return functools.partial(lax.fori_loop, 0, blocks // step, run)


def emit_packets(send_hot, squashed, packets):
    halo = packets[0].shape[0]
    sent = mm(send_hot[...], squashed[...]).astype(BF16)
    for d, packet in enumerate(packets):
        packet[...] = sent[d * halo : (d + 1) * halo]


def first_kernel(state, send_hot, squashed, *packets):
    comps, _, nodes = state.shape
    for c in range(comps):
        squashed[:, c * nodes : (c + 1) * nodes] = jnp.tanh(state[c]).astype(BF16)
    emit_packets(send_hot, squashed, packets)


def residual_products(squashed, received, gather_hot, lift, products):
    blocks = squashed.shape[0]
    slots, nodes, _ = lift.shape
    comps = squashed.shape[1] // nodes
    own = squashed[...]
    extended = jnp.concatenate([own] + [r[...] for r in received], axis=0)
    picked = mm(gather_hot[...], extended).astype(BF16)
    for k in range(slots):
        rows = own if k == 0 else picked[(k - 1) * blocks : k * blocks]
        stacked = jnp.concatenate([rows[:, c * nodes : (c + 1) * nodes] for c in range(comps)], axis=0)
        products[k] = mm_t(stacked, lift[k]).reshape(comps, blocks, nodes)


def stepped(rows, turn, mixing, state, sources, metric, products):
    slots, comps = products.shape[0], products.shape[1]
    totals = [None] * comps
    for k in range(slots):
        for c in range(comps):
            term = products[k, c, rows, :]
            for e in range(comps):
                part = mixing[(k * comps + e) * comps + c] * term
                totals[e] = part if totals[e] is None else totals[e] + part
    scale = metric[rows, :]
    return [
        state[e, rows, :]
        + STEP_SIZE
        * (turn[0] * sources[0, e, rows, :] + turn[1] * sources[1, e, rows, :] - scale * totals[e])
        for e in range(comps)
    ]


def forward_kernel(
    turn, mixing, state, squashed_in, r0, r1, r2, r3, sources, metric, lift, gather_hot, send_hot,
    next_state, squashed, p0, p1, p2, p3, products,
):
    comps, blocks, nodes = state.shape
    residual_products(squashed_in, (r0, r1, r2, r3), gather_hot, lift, products)

    def body(rows, carry):
        fresh = stepped(rows, turn, mixing, state, sources, metric, products)
        for e in range(comps):
            next_state[e, rows, :] = fresh[e]
            squashed[rows, e * nodes : (e + 1) * nodes] = jnp.tanh(fresh[e]).astype(BF16)
        return carry

    chunks(blocks, body)(0)
    emit_packets(send_hot, squashed, (p0, p1, p2, p3))


def mix_back(rows, turn, mixing, adjoint, sources, metric, mixed, grad):
    slots, comps = mixed.shape[0], mixed.shape[1]
    scale = metric[rows, :]
    for e in range(comps):
        turning = turn[0] * sources[1, e, rows, :] - turn[1] * sources[0, e, rows, :]
        part = adjoint[e] * turning
        grad = grad + part.reshape(-1, 8, part.shape[-1]).sum(axis=0)
    weighted = [scale * adjoint[e] for e in range(comps)]
    for k in range(slots):
        for c in range(comps):
            total = mixing[k * comps * comps + c] * weighted[0]
            for e in range(1, comps):
                total = total + mixing[(k * comps + e) * comps + c] * weighted[e]
            mixed[k, c, rows, :] = total.astype(BF16)
    return grad


def push_back(mixed, lift, scatter_hot, terms, local_part, packets):
    slots, comps, blocks, nodes = mixed.shape
    halo = packets[0].shape[0]
    own = None
    for k in range(slots):
        product = mm(mixed[k].reshape(comps * blocks, nodes), lift[k])
        if k == 0:
            own = product
            continue
        for c in range(comps):
            terms[(k - 1) * blocks : k * blocks, c * nodes : (c + 1) * nodes] = product[
                c * blocks : (c + 1) * blocks
            ].astype(BF16)
    totals = mm(scatter_hot[...], terms[...])
    for c in range(comps):
        local_part[:, c * nodes : (c + 1) * nodes] = (
            totals[:blocks, c * nodes : (c + 1) * nodes] + own[c * blocks : (c + 1) * blocks]
        )
    for d, packet in enumerate(packets):
        packet[...] = totals[blocks + d * halo : blocks + (d + 1) * halo].astype(BF16)


def turn_kernel(
    turn, mixing, state, squashed_in, r0, r1, r2, r3, sources, metric, weight, adjoint_end, lift,
    gather_hot, scatter_hot, adjoint, grad, local_part, p0, p1, p2, p3, products, mixed, terms,
):
    comps, blocks, nodes = state.shape
    residual_products(squashed_in, (r0, r1, r2, r3), gather_hot, lift, products)

    def body(rows, carry):
        fresh = stepped(rows, turn, mixing, state, sources, metric, products)
        values = [adjoint_end[e, rows, :] + weight[e, rows, :] * fresh[e] for e in range(comps)]
        for e in range(comps):
            adjoint[e, rows, :] = values[e]
        return mix_back(rows, turn, mixing, values, sources, metric, mixed, carry)

    grad[...] = chunks(blocks, body)(jnp.zeros(grad.shape, F32))
    push_back(mixed, lift, scatter_hot, terms, local_part, (p0, p1, p2, p3))


def start_kernel(
    turn, mixing, adjoint, sources, metric, lift, scatter_hot,
    grad, local_part, p0, p1, p2, p3, mixed, terms,
):
    comps, blocks, nodes = adjoint.shape

    def body(rows, carry):
        values = [adjoint[e, rows, :] for e in range(comps)]
        return mix_back(rows, turn, mixing, values, sources, metric, mixed, carry)

    grad[...] = chunks(blocks, body)(jnp.zeros(grad.shape, F32))
    push_back(mixed, lift, scatter_hot, terms, local_part, (p0, p1, p2, p3))


def finished(rows, keep, adjoint_in, pushed, state, weight):
    comps, _, nodes = adjoint_in.shape
    values = []
    for e in range(comps):
        now = state[e, rows, :]
        bent = jnp.tanh(now)
        values.append(
            adjoint_in[e, rows, :]
            - STEP_SIZE * (pushed[rows, e * nodes : (e + 1) * nodes] * (1.0 - bent * bent))
            + keep * (weight[e, rows, :] * now)
        )
    return values


def add_returned(local_in, received, return_hot, pushed):
    returned = jnp.concatenate([r[...] for r in received], axis=0)
    pushed[...] = local_in[...] + mm(return_hot[...], returned)


def reverse_kernel(
    turn, mixing, adjoint_in, local_in, r0, r1, r2, r3, state, weight, sources, metric, lift,
    scatter_hot, return_hot, adjoint, grad, local_part, p0, p1, p2, p3, pushed, mixed, terms,
):
    comps, blocks, nodes = state.shape
    add_returned(local_in, (r0, r1, r2, r3), return_hot, pushed)

    def body(rows, carry):
        values = finished(rows, 1.0, adjoint_in, pushed, state, weight)
        for e in range(comps):
            adjoint[e, rows, :] = values[e]
        return mix_back(rows, turn, mixing, values, sources, metric, mixed, carry)

    grad[...] = chunks(blocks, body)(jnp.zeros(grad.shape, F32))
    push_back(mixed, lift, scatter_hot, terms, local_part, (p0, p1, p2, p3))


def last_kernel(keep, adjoint_in, local_in, r0, r1, r2, r3, state, weight, return_hot, adjoint, pushed):
    comps, blocks, nodes = state.shape
    add_returned(local_in, (r0, r1, r2, r3), return_hot, pushed)

    def body(rows, carry):
        values = finished(rows, keep[0], adjoint_in, pushed, state, weight)
        for e in range(comps):
            adjoint[e, rows, :] = values[e]
        return carry

    chunks(blocks, body)(0)


def collect_kernel(count, factor, group, *refs):
    grads, spread = refs[:-1], refs[-1]
    phases = len(grads) // count
    lane = lax.broadcasted_iota(jnp.int32, (8, spread.shape[-1]), 1)
    total = jnp.zeros((8, spread.shape[-1]), F32)
    for n in range(count):
        chosen = grads[count - 1 - n][...]
        for step in range(1, phases):
            other = grads[step * count + count - 1 - n][...]
            chosen = jnp.where(group[0] == phases - 1 - step, other, chosen)
        summed = jnp.sum(chosen, axis=1, keepdims=True)
        total = jnp.where(lane == n, summed, total)
    row = jnp.sum(total, axis=0, keepdims=True) * factor
    spread[...] = jnp.broadcast_to(row[None], spread.shape)


def call(kernel, scalars, arrays, outs, scratch=()):
    smem = pl.BlockSpec(memory_space=pltpu.SMEM)
    vmem = pl.BlockSpec(memory_space=pltpu.VMEM)
    return pl.pallas_call(
        kernel,
        out_shape=outs,
        in_specs=[smem] * len(scalars) + [vmem] * len(arrays),
        out_specs=[vmem] * len(outs),
        scratch_shapes=[pltpu.VMEM(shape, dtype) for shape, dtype in scratch],
        compiler_params=pltpu.CompilerParams(vmem_limit_bytes=16 * 1024 * 1024),
        name=getattr(kernel, "func", kernel).__name__,
    )(*scalars, *arrays)


def swap(packets, sign):
    devices = range(lax.axis_size("space"))
    received = []
    for packet, offset in zip(packets, OFFSETS):
        route = [(i, (i + sign * offset) % len(devices)) for i in devices]
        received.append(lax.ppermute(packet, "space", route))
    return received


def shards(
    checkpoints, sources, pitch, metric, obj_weight, adjoint_end, lift, mixing, faces, send_idx
):
    comps, blocks, nodes = adjoint_end.shape
    slots = lift.shape[0]
    group = lax.axis_index("tm")
    groups = lax.axis_size("tm")
    count = pitch.shape[0] // groups
    halo = send_idx.shape[2]
    wide = comps * nodes
    extent = blocks + len(OFFSETS) * halo
    normalizer = math.sqrt(comps * nodes * blocks * lax.axis_size("space"))

    senders = send_idx.reshape(-1)
    named = faces.T.reshape(-1)
    place = lax.axis_index("space")
    width = lax.axis_size("space")
    column = jnp.arange(extent, dtype=jnp.int32)
    arrives = functools.reduce(jnp.logical_or, [
        (column >= blocks + d * halo) & (column < blocks + (d + 1) * halo)
        & ((place - o < 0) | (place - o >= width))
        for d, o in enumerate(OFFSETS)
    ])
    gather_hot = ((named[:, None] == column[None, :]) & ~arrives[None, :]).astype(BF16)
    scatter_hot = (named[None, :] == jnp.arange(extent, dtype=jnp.int32)[:, None]).astype(BF16)
    send_hot = (senders[:, None] == jnp.arange(blocks, dtype=jnp.int32)[None, :]).astype(BF16)
    slot = jnp.arange(len(OFFSETS) * halo, dtype=jnp.int32)
    returns = functools.reduce(jnp.logical_or, [
        (slot >= d * halo) & (slot < (d + 1) * halo) & (place + o >= 0) & (place + o < width)
        for d, o in enumerate(OFFSETS)
    ])
    return_hot = (
        (senders[None, :] == jnp.arange(blocks, dtype=jnp.int32)[:, None]) & returns[None, :]
    ).astype(BF16)
    own_pitch = lax.dynamic_slice_in_dim(pitch, group * count, count)
    turns = [jnp.stack([jnp.cos(own_pitch[n]), jnp.sin(own_pitch[n])]) for n in range(count)]
    mix_flat = mixing.reshape(-1)
    keep = (group > 0).astype(F32).reshape(1)

    def shape(dims, dtype=F32):
        return jax.ShapeDtypeStruct(dims, dtype)

    packet_shapes = [shape((halo, wide), BF16)] * len(OFFSETS)
    state_shape = shape((comps, blocks, nodes))
    reverse_shapes = [shape((8, nodes)), shape((blocks, wide))] + packet_shapes
    product_scratch = ((slots, comps, blocks, nodes), F32)
    push_scratch = [((slots, comps, blocks, nodes), BF16), (((slots - 1) * blocks, wide), BF16)]
    pushed_scratch = ((blocks, wide), F32)

    state = checkpoints[0]
    states = [state]
    squashed, *packets = call(
        first_kernel, (), (state, send_hot), [shape((blocks, wide), BF16)] + packet_shapes
    )
    for n in range(count - 1):
        received = swap(packets, 1)
        state, squashed, *packets = call(
            forward_kernel, (turns[n], mix_flat),
            (state, squashed, *received, sources, metric, lift, gather_hot, send_hot),
            [state_shape, shape((blocks, wide), BF16)] + packet_shapes, [product_scratch],
        )
        states.append(state)
    received = swap(packets, 1)
    adjoint, grad, local_part, *packets = call(
        turn_kernel, (turns[count - 1], mix_flat),
        (state, squashed, *received, sources, metric, obj_weight, adjoint_end, lift, gather_hot,
         scatter_hot),
        [state_shape] + reverse_shapes, [product_scratch] + push_scratch,
    )
    grads = []
    bound = None
    for phase in reversed(range(groups)):
        mine = group == phase
        if phase < groups - 1:
            adjoint = lax.ppermute(adjoint, "tm", [(phase + 1, phase)])
            grad, local_part, *packets = call(
                start_kernel, (turns[count - 1], mix_flat),
                (adjoint, sources, metric, lift, scatter_hot), reverse_shapes, push_scratch,
            )
        for n in reversed(range(count)):
            grads.append(grad)
            received = swap(packets, -1)
            if n > 0:
                adjoint, grad, local_part, *packets = call(
                    reverse_kernel, (turns[n - 1], mix_flat),
                    (adjoint, local_part, *received, states[n], obj_weight, sources, metric, lift,
                     scatter_hot, return_hot),
                    [state_shape] + reverse_shapes, [pushed_scratch] + push_scratch,
                )
            else:
                (adjoint,) = call(
                    last_kernel, (keep,),
                    (adjoint, local_part, *received, states[0], obj_weight, return_hot),
                    [state_shape], [pushed_scratch],
                )
        bound = adjoint if bound is None else jnp.where(mine, adjoint, bound)
    everyone = groups * width
    (spread,) = call(
        functools.partial(collect_kernel, count, STEP_SIZE / normalizer),
        (group.astype(jnp.int32).reshape(1),), grads, [shape((everyone, 1, nodes))],
    )
    every = lax.all_to_all(spread, ("tm", "space"), split_axis=0, concat_axis=0, tiled=True)
    values = every[:, 0, :count].reshape(groups, width, count).sum(axis=1).reshape(-1)
    return (bound[None], values)


def solution(mesh):
    placed = (
        P("tm", None, "space", None),
        P(None, None, "space", None),
        P(),
        P("space", None),
        P(None, "space", None),
        P(None, "space", None),
        P(),
        P(),
        P("space", None),
        P("space", None, None),
    )
    return jax.shard_map(
        shards,
        mesh=mesh,
        in_specs=placed,
        out_specs=(P("tm", None, "space", None), P()),
        check_vma=False,
    )
```

```python
import functools
import math

import jax
import jax.numpy as jnp
from jax import lax
from jax.experimental import pallas as pl
from jax.experimental.pallas import tpu as pltpu
from jax.sharding import PartitionSpec as P

OFFSETS = (1, -1, 2, -2)
STEP_SIZE = 0.5
CHUNK = 32
F32 = jnp.float32
BF16 = jnp.bfloat16


def mm(x, y):
    return lax.dot_general(x, y, (((1,), (0,)), ((), ())), preferred_element_type=F32)


def mm_t(x, y):
    return lax.dot_general(x, y, (((1,), (1,)), ((), ())), preferred_element_type=F32)


def chunks(blocks, body):
    step = math.gcd(blocks, CHUNK)

    def run(i, carry):
        return body(pl.ds(pl.multiple_of(i * step, step), step), carry)

    return functools.partial(lax.fori_loop, 0, blocks // step, run)


def emit_packets(send_hot, squashed, packets):
    halo = packets[0].shape[0]
    sent = mm(send_hot[...], squashed[...]).astype(BF16)
    for d, packet in enumerate(packets):
        packet[...] = sent[d * halo : (d + 1) * halo]


def first_kernel(state, send_hot, squashed, *packets):
    comps, _, nodes = state.shape
    for c in range(comps):
        squashed[:, c * nodes : (c + 1) * nodes] = jnp.tanh(state[c]).astype(BF16)
    emit_packets(send_hot, squashed, packets)


def residual_products(squashed, received, gather_hot, lift, products):
    blocks = squashed.shape[0]
    slots, nodes, _ = lift.shape
    comps = squashed.shape[1] // nodes
    own = squashed[...]
    extended = jnp.concatenate([own] + [r[...] for r in received], axis=0)
    picked = mm(gather_hot[...], extended).astype(BF16)
    for k in range(slots):
        rows = own if k == 0 else picked[(k - 1) * blocks : k * blocks]
        stacked = jnp.concatenate([rows[:, c * nodes : (c + 1) * nodes] for c in range(comps)], axis=0)
        products[k] = mm_t(stacked, lift[k]).reshape(comps, blocks, nodes)


def stepped(rows, turn, mixing, state, sources, metric, products):
    slots, comps = products.shape[0], products.shape[1]
    totals = [None] * comps
    for k in range(slots):
        for c in range(comps):
            term = products[k, c, rows, :]
            for e in range(comps):
                part = mixing[(k * comps + e) * comps + c] * term
                totals[e] = part if totals[e] is None else totals[e] + part
    scale = metric[rows, :]
    return [
        state[e, rows, :]
        + STEP_SIZE
        * (turn[0] * sources[0, e, rows, :] + turn[1] * sources[1, e, rows, :] - scale * totals[e])
        for e in range(comps)
    ]


def forward_kernel(
    turn, mixing, state, squashed_in, r0, r1, r2, r3, sources, metric, lift, gather_hot, send_hot,
    next_state, squashed, p0, p1, p2, p3, products,
):
    comps, blocks, nodes = state.shape
    residual_products(squashed_in, (r0, r1, r2, r3), gather_hot, lift, products)

    def body(rows, carry):
        fresh = stepped(rows, turn, mixing, state, sources, metric, products)
        for e in range(comps):
            next_state[e, rows, :] = fresh[e]
            squashed[rows, e * nodes : (e + 1) * nodes] = jnp.tanh(fresh[e]).astype(BF16)
        return carry

    chunks(blocks, body)(0)
    emit_packets(send_hot, squashed, (p0, p1, p2, p3))


def mix_back(rows, turn, mixing, adjoint, sources, metric, mixed, grad):
    slots, comps = mixed.shape[0], mixed.shape[1]
    scale = metric[rows, :]
    for e in range(comps):
        turning = turn[0] * sources[1, e, rows, :] - turn[1] * sources[0, e, rows, :]
        part = adjoint[e] * turning
        grad = grad + part.reshape(-1, 8, part.shape[-1]).sum(axis=0)
    weighted = [scale * adjoint[e] for e in range(comps)]
    for k in range(slots):
        for c in range(comps):
            total = mixing[k * comps * comps + c] * weighted[0]
            for e in range(1, comps):
                total = total + mixing[(k * comps + e) * comps + c] * weighted[e]
            mixed[k, c, rows, :] = total.astype(BF16)
    return grad


def push_back(mixed, lift, scatter_hot, terms, local_part, packets):
    slots, comps, blocks, nodes = mixed.shape
    halo = packets[0].shape[0]
    own = None
    for k in range(slots):
        product = mm(mixed[k].reshape(comps * blocks, nodes), lift[k])
        if k == 0:
            own = product
            continue
        for c in range(comps):
            terms[(k - 1) * blocks : k * blocks, c * nodes : (c + 1) * nodes] = product[
                c * blocks : (c + 1) * blocks
            ].astype(BF16)
    totals = mm(scatter_hot[...], terms[...])
    for c in range(comps):
        local_part[:, c * nodes : (c + 1) * nodes] = (
            totals[:blocks, c * nodes : (c + 1) * nodes] + own[c * blocks : (c + 1) * blocks]
        )
    for d, packet in enumerate(packets):
        packet[...] = totals[blocks + d * halo : blocks + (d + 1) * halo].astype(BF16)


def turn_kernel(
    turn, mixing, state, squashed_in, r0, r1, r2, r3, sources, metric, weight, adjoint_end, lift,
    gather_hot, scatter_hot, adjoint, grad, local_part, p0, p1, p2, p3, products, mixed, terms,
):
    comps, blocks, nodes = state.shape
    residual_products(squashed_in, (r0, r1, r2, r3), gather_hot, lift, products)

    def body(rows, carry):
        fresh = stepped(rows, turn, mixing, state, sources, metric, products)
        values = [adjoint_end[e, rows, :] + weight[e, rows, :] * fresh[e] for e in range(comps)]
        for e in range(comps):
            adjoint[e, rows, :] = values[e]
        return mix_back(rows, turn, mixing, values, sources, metric, mixed, carry)

    grad[...] = chunks(blocks, body)(jnp.zeros(grad.shape, F32))
    push_back(mixed, lift, scatter_hot, terms, local_part, (p0, p1, p2, p3))


def start_kernel(
    turn, mixing, adjoint, sources, metric, lift, scatter_hot,
    grad, local_part, p0, p1, p2, p3, mixed, terms,
):
    comps, blocks, nodes = adjoint.shape

    def body(rows, carry):
        values = [adjoint[e, rows, :] for e in range(comps)]
        return mix_back(rows, turn, mixing, values, sources, metric, mixed, carry)

    grad[...] = chunks(blocks, body)(jnp.zeros(grad.shape, F32))
    push_back(mixed, lift, scatter_hot, terms, local_part, (p0, p1, p2, p3))


def finished(rows, keep, adjoint_in, pushed, state, weight):
    comps, _, nodes = adjoint_in.shape
    values = []
    for e in range(comps):
        now = state[e, rows, :]
        bent = jnp.tanh(now)
        values.append(
            adjoint_in[e, rows, :]
            - STEP_SIZE * (pushed[rows, e * nodes : (e + 1) * nodes] * (1.0 - bent * bent))
            + keep * (weight[e, rows, :] * now)
        )
    return values


def add_returned(local_in, received, return_hot, pushed):
    returned = jnp.concatenate([r[...] for r in received], axis=0)
    pushed[...] = local_in[...] + mm(return_hot[...], returned)


def reverse_kernel(
    turn, mixing, adjoint_in, local_in, r0, r1, r2, r3, state, weight, sources, metric, lift,
    scatter_hot, return_hot, adjoint, grad, local_part, p0, p1, p2, p3, pushed, mixed, terms,
):
    comps, blocks, nodes = state.shape
    add_returned(local_in, (r0, r1, r2, r3), return_hot, pushed)

    def body(rows, carry):
        values = finished(rows, 1.0, adjoint_in, pushed, state, weight)
        for e in range(comps):
            adjoint[e, rows, :] = values[e]
        return mix_back(rows, turn, mixing, values, sources, metric, mixed, carry)

    grad[...] = chunks(blocks, body)(jnp.zeros(grad.shape, F32))
    push_back(mixed, lift, scatter_hot, terms, local_part, (p0, p1, p2, p3))


def last_kernel(keep, adjoint_in, local_in, r0, r1, r2, r3, state, weight, return_hot, adjoint, pushed):
    comps, blocks, nodes = state.shape
    add_returned(local_in, (r0, r1, r2, r3), return_hot, pushed)

    def body(rows, carry):
        values = finished(rows, keep[0], adjoint_in, pushed, state, weight)
        for e in range(comps):
            adjoint[e, rows, :] = values[e]
        return carry

    chunks(blocks, body)(0)


def collect_kernel(count, factor, group, *refs):
    grads, spread = refs[:-1], refs[-1]
    phases = len(grads) // count
    lane = lax.broadcasted_iota(jnp.int32, (8, spread.shape[-1]), 1)
    total = jnp.zeros((8, spread.shape[-1]), F32)
    for n in range(count):
        chosen = grads[count - 1 - n][...]
        for step in range(1, phases):
            other = grads[step * count + count - 1 - n][...]
            chosen = jnp.where(group[0] == phases - 1 - step, other, chosen)
        summed = jnp.sum(chosen, axis=1, keepdims=True)
        total = jnp.where(lane == n, summed, total)
    row = jnp.sum(total, axis=0, keepdims=True) * factor
    spread[...] = jnp.broadcast_to(row[None], spread.shape)


def call(kernel, scalars, arrays, outs, scratch=()):
    smem = pl.BlockSpec(memory_space=pltpu.SMEM)
    vmem = pl.BlockSpec(memory_space=pltpu.VMEM)
    return pl.pallas_call(
        kernel,
        out_shape=outs,
        in_specs=[smem] * len(scalars) + [vmem] * len(arrays),
        out_specs=[vmem] * len(outs),
        scratch_shapes=[pltpu.VMEM(shape, dtype) for shape, dtype in scratch],
        compiler_params=pltpu.CompilerParams(vmem_limit_bytes=16 * 1024 * 1024),
        name=getattr(kernel, "func", kernel).__name__,
    )(*scalars, *arrays)


def swap(packets, sign):
    devices = range(lax.axis_size("space"))
    received = [None] * len(packets)
    for d in sorted(range(len(packets)), key=lambda d: -abs(OFFSETS[d])):
        route = [(i, (i + sign * OFFSETS[d]) % len(devices)) for i in devices]
        received[d] = lax.ppermute(packets[d], "space", route)
    return received


def shards(
    checkpoints, sources, pitch, metric, obj_weight, adjoint_end, lift, mixing, faces, send_idx
):
    comps, blocks, nodes = adjoint_end.shape
    slots = lift.shape[0]
    group = lax.axis_index("tm")
    groups = lax.axis_size("tm")
    count = pitch.shape[0] // groups
    halo = send_idx.shape[2]
    wide = comps * nodes
    extent = blocks + len(OFFSETS) * halo
    normalizer = math.sqrt(comps * nodes * blocks * lax.axis_size("space"))

    senders = send_idx.reshape(-1)
    named = faces.T.reshape(-1)
    place = lax.axis_index("space")
    width = lax.axis_size("space")
    column = jnp.arange(extent, dtype=jnp.int32)
    arrives = functools.reduce(jnp.logical_or, [
        (column >= blocks + d * halo) & (column < blocks + (d + 1) * halo)
        & ((place - o < 0) | (place - o >= width))
        for d, o in enumerate(OFFSETS)
    ])
    gather_hot = ((named[:, None] == column[None, :]) & ~arrives[None, :]).astype(BF16)
    scatter_hot = (named[None, :] == jnp.arange(extent, dtype=jnp.int32)[:, None]).astype(BF16)
    send_hot = (senders[:, None] == jnp.arange(blocks, dtype=jnp.int32)[None, :]).astype(BF16)
    slot = jnp.arange(len(OFFSETS) * halo, dtype=jnp.int32)
    returns = functools.reduce(jnp.logical_or, [
        (slot >= d * halo) & (slot < (d + 1) * halo) & (place + o >= 0) & (place + o < width)
        for d, o in enumerate(OFFSETS)
    ])
    return_hot = (
        (senders[None, :] == jnp.arange(blocks, dtype=jnp.int32)[:, None]) & returns[None, :]
    ).astype(BF16)
    own_pitch = lax.dynamic_slice_in_dim(pitch, group * count, count)
    turns = [jnp.stack([jnp.cos(own_pitch[n]), jnp.sin(own_pitch[n])]) for n in range(count)]
    mix_flat = mixing.reshape(-1)
    keep = (group > 0).astype(F32).reshape(1)

    def shape(dims, dtype=F32):
        return jax.ShapeDtypeStruct(dims, dtype)

    packet_shapes = [shape((halo, wide), BF16)] * len(OFFSETS)
    state_shape = shape((comps, blocks, nodes))
    reverse_shapes = [shape((8, nodes)), shape((blocks, wide))] + packet_shapes
    product_scratch = ((slots, comps, blocks, nodes), F32)
    push_scratch = [((slots, comps, blocks, nodes), BF16), (((slots - 1) * blocks, wide), BF16)]
    pushed_scratch = ((blocks, wide), F32)

    state = checkpoints[0]
    states = [state]
    squashed, *packets = call(
        first_kernel, (), (state, send_hot), [shape((blocks, wide), BF16)] + packet_shapes
    )
    for n in range(count - 1):
        received = swap(packets, 1)
        state, squashed, *packets = call(
            forward_kernel, (turns[n], mix_flat),
            (state, squashed, *received, sources, metric, lift, gather_hot, send_hot),
            [state_shape, shape((blocks, wide), BF16)] + packet_shapes, [product_scratch],
        )
        states.append(state)
    received = swap(packets, 1)
    adjoint, grad, local_part, *packets = call(
        turn_kernel, (turns[count - 1], mix_flat),
        (state, squashed, *received, sources, metric, obj_weight, adjoint_end, lift, gather_hot,
         scatter_hot),
        [state_shape] + reverse_shapes, [product_scratch] + push_scratch,
    )
    grads = []
    bound = None
    for phase in reversed(range(groups)):
        mine = group == phase
        if phase < groups - 1:
            adjoint = lax.ppermute(adjoint, "tm", [(phase + 1, phase)])
            grad, local_part, *packets = call(
                start_kernel, (turns[count - 1], mix_flat),
                (adjoint, sources, metric, lift, scatter_hot), reverse_shapes, push_scratch,
            )
        for n in reversed(range(count)):
            grads.append(grad)
            received = swap(packets, -1)
            if n > 0:
                adjoint, grad, local_part, *packets = call(
                    reverse_kernel, (turns[n - 1], mix_flat),
                    (adjoint, local_part, *received, states[n], obj_weight, sources, metric, lift,
                     scatter_hot, return_hot),
                    [state_shape] + reverse_shapes, [pushed_scratch] + push_scratch,
                )
            else:
                (adjoint,) = call(
                    last_kernel, (keep,),
                    (adjoint, local_part, *received, states[0], obj_weight, return_hot),
                    [state_shape], [pushed_scratch],
                )
        bound = adjoint if bound is None else jnp.where(mine, adjoint, bound)
    everyone = groups * width
    (spread,) = call(
        functools.partial(collect_kernel, count, STEP_SIZE / normalizer),
        (group.astype(jnp.int32).reshape(1),), grads, [shape((everyone, 1, nodes))],
    )
    every = lax.all_to_all(spread, ("tm", "space"), split_axis=0, concat_axis=0, tiled=True)
    values = every[:, 0, :count].reshape(groups, width, count).sum(axis=1).reshape(-1)
    return (bound[None], values)


def solution(mesh):
    placed = (
        P("tm", None, "space", None),
        P(None, None, "space", None),
        P(),
        P("space", None),
        P(None, "space", None),
        P(None, "space", None),
        P(),
        P(),
        P("space", None),
        P("space", None, None),
    )
    return jax.shard_map(
        shards,
        mesh=mesh,
        in_specs=placed,
        out_specs=(P("tm", None, "space", None), P()),
        check_vma=False,
    )
```
